128 devices in a mesh: lat: 8 (over y_hi, z), lon: 16 (over x, y_lo, core).
Axes of the slice: x: 4, y: 4 (y_hi: 2, y_lo: 2; y = y_hi * 2 + y_lo), z: 4, core: 2. Of those that a mesh axis runs over, the one named last changes fastest.
Arguments:
- fields: bfloat16 [2, 256, 768, 256], P(None, 'lat', 'lon'), may hold values from -6 to 6
- kernel: bfloat16 [9, 256, 256], replicated, may hold values from -0.125 to 0.125
- conv_bias: float32 [256], replicated, may hold values from -3 to 3
- cotangent: bfloat16 [2, 128, 384, 256], P(None, 'lat', 'lon'), may hold values from -6 to 6
Outputs:
- pooled: bfloat16 [2, 128, 384, 256], P(None, 'lat', 'lon')
- grad_input: bfloat16 [2, 256, 768, 256], P(None, 'lat', 'lon')
- grad_kernel: float32 [9, 256, 256], replicated
- grad_bias: float32 [256], replicated
The draws below stay inside these ranges and needn't reach their ends.
All inputs are finite; a program needn't handle non-finite values.
Results may differ from the reference program's by a relative error of at most 0.013.
Values may be sent and summed in bfloat16 or wider, within the bound.
No kernel may reach another device: no remote copies, remote signals or barrier semaphores. Data moves between devices by JAX's collectives and lax.ppermute only.
A program may use at most 64 MiB of HBM per device.

```python
import math
import jax
import jax.numpy as jnp
from jax import lax

CHANNELS = 256
BATCH = 2
NLAT = 256
NLON = 768


def shard_levels(key, extent, cuts, smallest, high):
    gain, own = 1.0, jax.random.fold_in(key, 6)
    for axis_at, parts in cuts:
        steps = jnp.exp(jax.random.uniform(jax.random.fold_in(own, axis_at), (parts,), jnp.float32, smallest / len(cuts), high / len(cuts)))
        gain = gain * jnp.repeat(steps, extent[axis_at] // parts).reshape([-1 if axis == axis_at else 1 for axis in range(len(extent))])
    return gain


def gaussian(key, dims, deviation, bound, split=(), dtype=jnp.bfloat16):
    entries = deviation * jax.random.normal(key, dims, jnp.float32)
    if split:
        entries = entries * shard_levels(key, dims, split, -0.22, 0.18)
    return jnp.clip(entries, -bound, bound).astype(dtype)


def setup_inputs(seed: int = 0) -> dict:
    seeds = jax.random.split(jax.random.key(seed), 5)
    fields = gaussian(seeds[0], (BATCH, NLAT, NLON, CHANNELS), 1.0, 6.0, ((1, 8), (2, 16)))
    kernel = gaussian(seeds[1], (9, CHANNELS, CHANNELS), (9 * CHANNELS) ** -0.5, 0.125)
    conv_bias = gaussian(seeds[2], (CHANNELS,), 0.5, 3.0, (), jnp.float32)
    cotangent = gaussian(seeds[3], (BATCH, NLAT // 2, NLON // 2, CHANNELS), 1.0, 6.0, ((1, 8), (2, 16)))
    return {"fields": fields, "kernel": kernel, "conv_bias": conv_bias, "cotangent": cotangent}


def lat_cosine(rows, first, total):
    index_rows = (first + jnp.arange(rows)).astype(jnp.float32)
    return jnp.cos((index_rows + 0.5) * (math.pi / total) - math.pi / 2)

def polar_pad(field):
    north_row = jnp.roll(field[:, :1], NLON // 2, axis=2)
    south_row = jnp.roll(field[:, -1:], NLON // 2, axis=2)
    tall = jnp.concatenate([north_row, field, south_row], axis=1)
    return jnp.concatenate([tall[:, :, -1:], tall, tall[:, :, :1]], axis=2)

def forward_conv(padded, kernel, rows, cols):
    chans = padded.shape[-1]
    total = jnp.zeros((padded.shape[0] * rows * cols, kernel.shape[2]), jnp.float32)
    for row_off in range(3):
        for col_off in range(3):
            window = padded[:, row_off:row_off + rows, col_off:col_off + cols, :].reshape(-1, chans)
            total = total + jnp.dot(window, kernel[3 * row_off + col_off], preferred_element_type=jnp.float32)
    return total.reshape(padded.shape[0], rows, cols, kernel.shape[2])

def back_conv(padded, kernel, rows, cols):
    chans = padded.shape[-1]
    total = jnp.zeros((padded.shape[0] * rows * cols, kernel.shape[1]), jnp.float32)
    for row_off in range(3):
        for col_off in range(3):
            window = padded[:, 2 - row_off:2 - row_off + rows, 2 - col_off:2 - col_off + cols, :].reshape(-1, chans)
            total = total + lax.dot_general(window, kernel[3 * row_off + col_off], (((1,), (1,)), ((), ())), preferred_element_type=jnp.float32)
    return total.reshape(padded.shape[0], rows, cols, kernel.shape[1])

def pole_term(pad_row, kernel, row_off, cols):
    chans = pad_row.shape[-1]
    total = jnp.zeros((pad_row.shape[0] * cols, kernel.shape[1]), jnp.float32)
    for col_off in range(3):
        window = pad_row[:, :, 2 - col_off:2 - col_off + cols, :].reshape(-1, chans)
        total = total + lax.dot_general(window, kernel[3 * row_off + col_off], (((1,), (1,)), ((), ())), preferred_element_type=jnp.float32)
    return total.reshape(pad_row.shape[0], 1, cols, kernel.shape[1])

def kernel_grad(padded, grad_pre, rows, cols):
    chans = padded.shape[-1]
    flat_grad = grad_pre.reshape(-1, grad_pre.shape[-1])
    pieces = []
    for row_off in range(3):
        for col_off in range(3):
            window = padded[:, row_off:row_off + rows, col_off:col_off + cols, :].reshape(-1, chans)
            pieces.append(lax.dot_general(window, flat_grad, (((0,), (0,)), ((), ())), preferred_element_type=jnp.float32))
    return jnp.stack(pieces, axis=0)

def reference(fields, kernel, conv_bias, cotangent):
    batches, rows, cols, chans = fields.shape
    padded = polar_pad(fields)
    pre = forward_conv(padded, kernel, rows, cols) + conv_bias.astype(jnp.float32)
    sigma = jax.nn.sigmoid(pre)
    active = (pre * sigma).astype(jnp.bfloat16)
    cosine = lat_cosine(rows, 0, NLAT)
    pair_sum = cosine[0::2] + cosine[1::2]
    weighted = active.astype(jnp.float32) * cosine[None, :, None, None]
    pooled = weighted.reshape(batches, rows // 2, 2, cols // 2, 2, chans).sum(axis=(2, 4)) / (2.0 * pair_sum)[None, :, None, None]
    share = cosine / (2.0 * jnp.repeat(pair_sum, 2))
    spread = jnp.repeat(jnp.repeat(cotangent.astype(jnp.float32), 2, axis=1), 2, axis=2)
    grad_pre = (spread * share[None, :, None, None] * sigma * (1.0 + pre * (1.0 - sigma))).astype(jnp.bfloat16)
    grad_bias = lax.optimization_barrier(jnp.sum(grad_pre.astype(jnp.float32), axis=(0, 1, 2)))
    grad_kernel = kernel_grad(padded, grad_pre, rows, cols)
    grad_padded = polar_pad(grad_pre)
    blank = jnp.zeros_like(grad_padded[:, :1])
    inner = jnp.concatenate([blank, grad_padded[:, 1:-1], blank], axis=1)
    back = back_conv(inner, kernel, rows, cols)
    north_add = pole_term(grad_padded[:, :1], kernel, 0, cols)
    south_add = pole_term(grad_padded[:, -1:], kernel, 2, cols)
    back = jnp.concatenate([back[:, :1] + north_add, back[:, 1:-1], back[:, -1:] + south_add], axis=1)
    return (pooled.astype(jnp.bfloat16), back.astype(jnp.bfloat16), grad_kernel, grad_bias)
```

```python
import math

import jax
import jax.numpy as jnp
from jax import lax
from jax.experimental import pallas as pl
from jax.experimental.pallas import tpu as pltpu
from jax.sharding import Mesh, PartitionSpec as P

F32 = jnp.float32
BF16 = jnp.bfloat16
LAT = ("yh", "z")
LON = ("x", "yl", "core")
RING = ("yh", "yl")
PLANE = ("x", "z")


def edge_block(right0, right1, left0, left1, chans):
    place = lax.broadcasted_iota(jnp.int32, (8, chans), 0)
    return jnp.where(
        place == 0,
        right0,
        jnp.where(place == 1, right1, jnp.where(place == 6, left0, jnp.where(place == 7, left1, 0.0))),
    )


def forward_kernel(
    flags, share, field, from_fore, from_aft, from_right, from_left, cot, weights, bias,
    pooled, grad, keep, give, wide, right, left, spread, pool, flipped, total, bias_total,
):
    batches, rows, cols, chans = field.shape
    width = cols + 8
    pairs = rows // 2
    step = 8
    is_north, is_south, first_half, core = flags[0], flags[1], flags[2], flags[3]
    right[...] = from_right[...].astype(F32)
    left[...] = from_left[...].astype(F32)
    span = rows + 4

    def put(b, e, own):
        edge = edge_block(
            right[b, pl.ds(e, 1), :], right[b, pl.ds(span + e, 1), :],
            left[b, pl.ds(e, 1), :], left[b, pl.ds(span + e, 1), :], chans,
        )
        line = jnp.concatenate([own, edge], axis=0)
        wide[b, e, :, :chans] = pltpu.roll(line, 1, 0).astype(BF16)
        wide[b, e, :, chans : 2 * chans] = line.astype(BF16)
        wide[b, e, :, 2 * chans :] = pltpu.roll(line, width - 1, 0).astype(BF16)

    def halo(b, lo, hi):
        fore = from_fore[b, lo:hi, :].astype(F32)
        aft = from_aft[b, lo:hi, :].astype(F32)
        top = jnp.where(first_half == 1, fore, aft)
        bottom = jnp.where(first_half == 1, aft, fore)
        return top, bottom

    for b in range(batches):
        for k in range(2):
            top, bottom = halo(b, k * cols, (k + 1) * cols)
            put(b, k, top)
            put(b, rows + 2 + k, bottom)

        def fill(i, carry):
            put(b, i + 2, field[b, i].astype(F32))
            return carry

        lax.fori_loop(0, rows, fill, 0, unroll=4)

    def conv(parts):
        acc = None
        for r in range(3):
            term = jnp.dot(parts[r], weights[r], preferred_element_type=F32)
            acc = term if acc is None else acc + term
        return acc + bias[...]

    def slope(pre):
        sigma = 1.0 / (1.0 + jnp.exp(-pre))
        return sigma, sigma * (1.0 + pre * (1.0 - sigma))

    def join(ref, slot, at):
        return jnp.concatenate([ref[slot, h, at, :] for h in range(chans // 128)], axis=-1)

    def lift(slot, b, q, own):
        for h in range(chans // 128):
            for k in range(2):
                spread[slot, h, pl.ds(k, cols // 2, stride=2), :] = own[:, h * 128 : h * 128 + 128]
        place = lax.broadcasted_iota(jnp.int32, (8, chans), 0)
        edge = jnp.where(
            place == 0,
            right[b, pl.ds(2 * span + q, 1), :],
            jnp.where(place == 7, left[b, pl.ds(2 * span + q, 1), :], 0.0),
        )
        return jnp.concatenate([join(spread, slot, slice(0, cols)), edge], axis=0)

    for t in range(2):
        base = 0 if t == 0 else rows + 1
        turned = is_north if t == 0 else is_south
        parts = []
        for r in range(3):
            at = base + jnp.where(turned == 1, 2 - r, r)
            parts.append(wide[:, pl.ds(at, 1), :, :].reshape(batches * width, 3 * chans))
        _, rate = slope(conv(parts))
        for b in range(batches):
            cot_rows = halo(b, 2 * cols, 2 * cols + cols // 2)[t]
            value = lift(0, b, 0 if t == 0 else pairs + 1, cot_rows) * share[0 if t == 0 else rows + 1] * rate[b * width : (b + 1) * width]
            grad[b, 0 if t == 0 else rows + 1] = value.astype(BF16)

    bias_total[...] = jnp.zeros_like(bias_total)
    blocks = rows // step

    def block(n, carry):
        b = n // blocks
        first = (n % blocks) * step
        parts = [
            wide[b, pl.ds(first + 1 + r, step), :, :].reshape(step * width, 3 * chans) for r in range(3)
        ]
        pre = conv(parts)
        sigma, rate = slope(pre)
        active = (pre * sigma).astype(BF16).astype(F32).reshape(step, width, chans)
        rate = rate.reshape(step, width, chans)
        lines = []
        for m in range(step // 2):
            q = first // 2 + m
            up, low = share[first + 2 * m + 1], share[first + 2 * m + 2]
            mixed = (active[2 * m] * up + active[2 * m + 1] * low)[:cols]
            for h in range(chans // 128):
                pool[m, h] = mixed[:, h * 128 : h * 128 + 128]
            even, odd = (join(pool, m, pl.ds(k, cols // 2, stride=2)) for k in range(2))
            pooled[b, q] = (even + odd).astype(BF16)
            lifted = lift(m, b, q + 1, cot[b, q].astype(F32))
            for k, part in ((2 * m, up), (2 * m + 1, low)):
                value = (lifted * part * rate[k]).astype(BF16)
                grad[b, first + k + 1] = value
                lines.append(value[:cols])
        own = jnp.concatenate(lines, axis=0)
        bias_total[...] += own.astype(F32).reshape(-1, 8, chans).sum(axis=0)
        at = pl.multiple_of(n * (step * cols), 128)
        flipped[:, pl.ds(at, step * cols)] = own.T
        return carry

    lax.fori_loop(0, batches * blocks, block, 0)

    size = rows * cols
    for r in range(3):
        acc = None
        for b in range(batches):
            term = jnp.dot(
                flipped[:, b * size : (b + 1) * size],
                wide[b, 1 + r : 1 + r + rows, :cols, :].reshape(size, 3 * chans),
                preferred_element_type=F32,
            )
            acc = term if acc is None else acc + term
        total[r * 3 * chans : (r + 1) * 3 * chans, :] = acc.T
    bias_sum = bias_total[...].sum(axis=0, keepdims=True)
    place = lax.broadcasted_iota(jnp.int32, (8, chans), 0)
    parts_count, deep = keep.shape[0], keep.shape[1] - 8
    for ref, side in ((keep, core), (give, 1 - core)):
        for j in range(parts_count):
            at = pl.multiple_of((side * parts_count + j) * deep, 8)
            ref[j, :deep, :] = total[pl.ds(at, deep), :].astype(ref.dtype)
            tail = jnp.where((place == 0) & (side == 0), bias_sum, 0.0) if j == 0 else jnp.zeros((8, chans), F32)
            ref[j, deep:, :] = tail.astype(ref.dtype)


def back_kernel(flags, grad, weights, out, wide, ends, acc):
    batches, slots, width, chans = grad.shape
    rows, cols = slots - 2, width - 8
    step = 8
    is_north, is_south = flags[0], flags[1]

    def put(line, ref, index):
        line = line.astype(F32)
        ref[(*index, slice(None), slice(0, chans))] = pltpu.roll(line, 1, 0)[:cols].astype(BF16)
        ref[(*index, slice(None), slice(chans, 2 * chans))] = line[:cols].astype(BF16)
        ref[(*index, slice(None), slice(2 * chans, 3 * chans))] = pltpu.roll(line, width - 1, 0)[:cols].astype(BF16)

    for b in range(batches):
        put(grad[b, 0], ends, (0, b))
        put(grad[b, slots - 1], ends, (1, b))
        wide[b, 0] = jnp.zeros_like(wide[b, 0])
        wide[b, slots - 1] = jnp.zeros_like(wide[b, slots - 1])

        def fill(i, carry):
            put(grad[b, i + 1], wide, (b, i + 1))
            return carry

        lax.fori_loop(0, rows, fill, 0, unroll=4)

    for t in range(2):
        tap = jnp.where(is_north == 1, 0, 2) if t == 0 else jnp.where(is_south == 1, 2, 0)
        lines = ends[t].reshape(batches * cols, 3 * chans)
        acc[t] = jnp.dot(lines, weights[tap], preferred_element_type=F32).reshape(batches, cols, chans)

    for b in range(batches):
        for first in range(0, rows, step):
            total = None
            for r in range(3):
                lines = wide[b, first + 2 - r : first + 2 - r + step, :, :].reshape(step * cols, 3 * chans)
                term = jnp.dot(lines, weights[r], preferred_element_type=F32)
                total = term if total is None else total + term
            total = total.reshape(step, cols, chans)
            for k in range(step):
                line = total[k]
                if first + k == 0:
                    line = line + acc[0, b]
                if first + k == rows - 1:
                    line = line + acc[1, b]
                out[b, first + k] = line.astype(BF16)


def circle(lats, lons):
    half = lons // 2
    fore = []
    for a in range(lats):
        for l in range(lons):
            if l < half:
                to = (a + 1, l) if a < lats - 1 else (a, l + half)
            else:
                to = (a - 1, l) if a > 0 else (a, l - half)
            fore.append((a * lons + l, to[0] * lons + to[1]))
    return fore, [(j, i) for i, j in fore]


def row_pair(field, at0, at1):
    return jnp.concatenate(
        [lax.dynamic_slice_in_dim(field, at0, 1, 1), lax.dynamic_slice_in_dim(field, at1, 1, 1)], axis=1
    )


def vmem():
    return pl.BlockSpec(memory_space=pltpu.VMEM)


def local(fields, kernel, conv_bias, cotangent):
    batches, rows, cols, chans = fields.shape
    lat_count, lon_count = lax.axis_size(LAT), lax.axis_size(LON)
    lat, lon = lax.axis_index(LAT), lax.axis_index(LON)
    first_half = lon < lon_count // 2
    is_north, is_south = lat == 0, lat == lat_count - 1
    pairs, halves = rows // 2, cols // 2

    low = (jnp.where(is_south, rows - 1, rows - 2), jnp.where(is_south, rows - 2, rows - 1), pairs - 1)
    high = (jnp.where(is_north, 1, 0), jnp.where(is_north, 0, 1), 0)

    def message(down):
        at = [jnp.where(down, x, y) for x, y in zip(low, high)]
        return jnp.concatenate(
            [
                row_pair(fields, at[0], at[1]).reshape(batches, 2 * cols, chans),
                lax.dynamic_slice_in_dim(cotangent, at[2], 1, 1).reshape(batches, halves, chans),
            ],
            axis=1,
        )

    fore, aft = circle(lat_count, lon_count)
    from_fore = lax.ppermute(message(first_half), LAT + LON, fore)
    from_aft = lax.ppermute(message(~first_half), LAT + LON, aft)
    top = jnp.where(first_half, from_fore, from_aft)
    bottom = jnp.where(first_half, from_aft, from_fore)

    def column(c):
        return [
            top[:, c : c + 1], top[:, cols + c : cols + c + 1], fields[:, :, c],
            bottom[:, c : c + 1], bottom[:, cols + c : cols + c + 1],
        ]

    def cot_column(c):
        at = 2 * cols + c
        return [top[:, at : at + 1], cotangent[:, :, c], bottom[:, at : at + 1]]

    to_left = jnp.concatenate(column(0) + column(1) + cot_column(0), axis=1)
    to_right = jnp.concatenate(column(cols - 2) + column(cols - 1) + cot_column(halves - 1), axis=1)
    ring = [(i, (i + 1) % lon_count) for i in range(lon_count)]
    from_left = lax.ppermute(to_right, LON, ring)
    from_right = lax.ppermute(to_left, LON, [(j, i) for i, j in ring])

    total_rows = rows * lat_count
    index = jnp.clip(lat * rows - 1 + jnp.arange(rows + 2), 0, total_rows - 1)

    def cosine(at):
        return jnp.cos((at.astype(F32) + 0.5) * (math.pi / total_rows) - math.pi / 2)

    even = index // 2 * 2
    share = cosine(index) / (2.0 * (cosine(even) + cosine(even + 1)))
    core = lax.axis_index("core")
    flags = jnp.stack([is_north, is_south, first_half, core == 1]).astype(jnp.int32)

    weights = kernel.reshape(3, 3 * chans, chans)
    back_weights = jnp.swapaxes(kernel.reshape(3, 3, chans, chans)[:, ::-1], 2, 3).reshape(3, 3 * chans, chans)
    plane = lax.axis_size(PLANE)
    deep = 9 * chans // (2 * plane)
    smem = pl.BlockSpec(memory_space=pltpu.SMEM)
    message_type = jax.ShapeDtypeStruct((plane, deep + 8, chans), BF16)
    count = from_right.shape[1]
    pooled, grad, keep, give = pl.pallas_call(
        forward_kernel,
        out_shape=(
            jax.ShapeDtypeStruct((batches, pairs, halves, chans), BF16),
            jax.ShapeDtypeStruct((batches, rows + 2, cols + 8, chans), BF16),
            message_type,
            message_type,
        ),
        in_specs=[smem, smem] + [vmem()] * 8,
        out_specs=[vmem()] * 4,
        scratch_shapes=[
            pltpu.VMEM((batches, rows + 4, cols + 8, 3 * chans), BF16),
            pltpu.VMEM((batches, count, chans), F32),
            pltpu.VMEM((batches, count, chans), F32),
            pltpu.VMEM((4, chans // 128, cols, 128), F32),
            pltpu.VMEM((4, chans // 128, cols, 128), F32),
            pltpu.VMEM((chans, batches * rows * cols), BF16),
            pltpu.VMEM((9 * chans, chans), F32),
            pltpu.VMEM((8, chans), F32),
        ],
        name="forward",
    )(flags, share, fields, from_fore, from_aft, from_right, from_left, cotangent, weights, conv_bias[None])

    back = pl.pallas_call(
        back_kernel,
        out_shape=jax.ShapeDtypeStruct((batches, rows, cols, chans), BF16),
        in_specs=[smem, vmem(), vmem()],
        out_specs=vmem(),
        scratch_shapes=[
            pltpu.VMEM((batches, rows + 2, cols, 3 * chans), BF16),
            pltpu.VMEM((2, batches, cols, 3 * chans), BF16),
            pltpu.VMEM((2, batches, cols, chans), F32),
        ],
        name="back",
    )(flags, grad, back_weights)

    take = lax.ppermute(give, "core", [(0, 1), (1, 0)])
    part = (keep.astype(F32) + take.astype(F32)).astype(BF16)
    part = lax.all_to_all(part, PLANE, 0, 0, tiled=True)
    part = part.astype(F32).sum(axis=0).astype(BF16)
    size = lax.axis_size(RING)
    total = part.astype(F32)
    for k in range(1, size):
        total = total + lax.ppermute(part, RING, [(i, (i + k) % size) for i in range(size)]).astype(F32)
    total = jnp.broadcast_to(total.astype(BF16)[None], (plane, deep + 8, chans))
    total = lax.all_to_all(total, PLANE, 0, 0, tiled=True)
    total = lax.all_gather(total, "core", axis=0, tiled=True)
    grad_kernel = total[:, :deep].astype(F32).reshape(9, chans, chans)
    grad_bias = total[0, deep].astype(F32)
    return pooled, back, grad_kernel, grad_bias


def solution(mesh):
    lats, lons = mesh.devices.shape
    fine = Mesh(mesh.devices.reshape(2, lats // 2, lons // 4, 2, 2), LAT + LON)
    spec = P(None, LAT, LON, None)
    return jax.shard_map(
        local,
        mesh=fine,
        in_specs=(spec, P(), P(), spec),
        out_specs=(spec, spec, P(), P()),
        check_vma=False,
    )
```

```python
import functools
import math

import jax
import jax.numpy as jnp
from jax import lax
from jax.experimental import pallas as pl
from jax.experimental.pallas import tpu as pltpu
from jax.sharding import Mesh, PartitionSpec as P


F32 = jnp.float32
BF16 = jnp.bfloat16
HALVES = 2
LAT = ("yh", "z")
LON = ("x", "yl", "core")
RING = ("yh", "yl")
PLANE = ("x", "z")


def edge_block(right0, right1, left0, left1, chans):
    place = lax.broadcasted_iota(jnp.int32, (8, chans), 0)
    return jnp.where(
        place == 0,
        right0,
        jnp.where(place == 1, right1, jnp.where(place == 6, left0, jnp.where(place == 7, left1, 0.0))),
    )


def forward_kernel(
    flags, share, field, from_fore, from_aft, from_right, from_left, cot, weights, bias,
    pooled, grad, keep, give, wide, right, left, spread, pool, flipped, total, bias_total,
):
    batches, rows, cols, chans = field.shape
    width = cols + 8
    pairs = rows // 2
    step = 8
    is_north, is_south, first_half, core = flags[0], flags[1], flags[2], flags[3]
    right[...] = from_right[...].astype(F32)
    left[...] = from_left[...].astype(F32)
    span = rows + 4

    def put(b, e, own):
        edge = edge_block(
            right[b, pl.ds(e, 1), :], right[b, pl.ds(span + e, 1), :],
            left[b, pl.ds(e, 1), :], left[b, pl.ds(span + e, 1), :], chans,
        )
        line = jnp.concatenate([own, edge], axis=0)
        wide[b, e, :, :chans] = pltpu.roll(line, 1, 0).astype(BF16)
        wide[b, e, :, chans : 2 * chans] = line.astype(BF16)
        wide[b, e, :, 2 * chans :] = pltpu.roll(line, width - 1, 0).astype(BF16)

    def halo(b, lo, hi):
        fore = from_fore[b, lo:hi, :].astype(F32)
        aft = from_aft[b, lo:hi, :].astype(F32)
        top = jnp.where(first_half == 1, fore, aft)
        bottom = jnp.where(first_half == 1, aft, fore)
        return top, bottom

    for b in range(batches):
        for k in range(2):
            top, bottom = halo(b, k * cols, (k + 1) * cols)
            put(b, k, top)
            put(b, rows + 2 + k, bottom)

        def fill(i, carry):
            put(b, i + 2, field[b, i].astype(F32))
            return carry

        lax.fori_loop(0, rows, fill, 0, unroll=4)

    def conv(parts):
        acc = None
        for r in range(3):
            term = jnp.dot(parts[r], weights[r], preferred_element_type=F32)
            acc = term if acc is None else acc + term
        return acc + bias[...]

    def slope(pre):
        sigma = 0.5 + 0.5 * jnp.tanh(0.5 * pre)
        return sigma, sigma * (1.0 + pre * (1.0 - sigma))

    def join(ref, slot, at):
        return jnp.concatenate([ref[slot, h, at, :] for h in range(chans // 128)], axis=-1)

    def lift(slot, b, q, own):
        for h in range(chans // 128):
            for k in range(2):
                spread[slot, h, pl.ds(k, cols // 2, stride=2), :] = own[:, h * 128 : h * 128 + 128]
        place = lax.broadcasted_iota(jnp.int32, (8, chans), 0)
        edge = jnp.where(
            place == 0,
            right[b, pl.ds(2 * span + q, 1), :],
            jnp.where(place == 7, left[b, pl.ds(2 * span + q, 1), :], 0.0),
        )
        return jnp.concatenate([join(spread, slot, slice(0, cols)), edge], axis=0)

    for t in range(2):
        base = 0 if t == 0 else rows + 1
        turned = is_north if t == 0 else is_south
        parts = []
        for r in range(3):
            at = base + jnp.where(turned == 1, 2 - r, r)
            parts.append(wide[:, pl.ds(at, 1), :, :].reshape(batches * width, 3 * chans))
        _, rate = slope(conv(parts))
        for b in range(batches):
            cot_rows = halo(b, 2 * cols, 2 * cols + cols // 2)[t]
            value = lift(0, b, 0 if t == 0 else pairs + 1, cot_rows) * share[0 if t == 0 else rows + 1] * rate[b * width : (b + 1) * width]
            grad[b, 0 if t == 0 else rows + 1] = value.astype(BF16)

    bias_total[...] = jnp.zeros_like(bias_total)
    blocks = rows // step

    def block(n, carry):
        b = n // blocks
        first = (n % blocks) * step
        parts = [
            wide[b, pl.ds(first + 1 + r, step), :, :].reshape(step * width, 3 * chans) for r in range(3)
        ]
        pre = conv(parts)
        sigma, rate = slope(pre)
        active = (pre * sigma).reshape(step, width, chans)
        rate = rate.reshape(step, width, chans)
        lines = []
        for m in range(step // 2):
            q = first // 2 + m
            up, low = share[first + 2 * m + 1], share[first + 2 * m + 2]
            mixed = (active[2 * m] * up + active[2 * m + 1] * low)[:cols]
            for h in range(chans // 128):
                pool[m, h] = mixed[:, h * 128 : h * 128 + 128]
            even, odd = (join(pool, m, pl.ds(k, cols // 2, stride=2)) for k in range(2))
            pooled[b, q] = (even + odd).astype(BF16)
            lifted = lift(m, b, q + 1, cot[b, q].astype(F32))
            for k, part in ((2 * m, up), (2 * m + 1, low)):
                value = (lifted * part * rate[k]).astype(BF16)
                grad[b, first + k + 1] = value
                lines.append(value[:cols])
        own = jnp.concatenate(lines, axis=0)
        bias_total[...] += own.astype(F32).reshape(-1, 8, chans).sum(axis=0)
        at = pl.multiple_of(n * (step * cols), 128)
        flipped[:, pl.ds(at, step * cols)] = own.T
        return carry

    lax.fori_loop(0, batches * blocks, block, 0, unroll=True)

    size = rows * cols
    for r in range(3):
        acc = None
        for b in range(batches):
            term = jnp.dot(
                flipped[:, b * size : (b + 1) * size],
                wide[b, 1 + r : 1 + r + rows, :cols, :].reshape(size, 3 * chans),
                preferred_element_type=F32,
            )
            acc = term if acc is None else acc + term
        total[r * 3 * chans : (r + 1) * 3 * chans, :] = acc.T
    bias_sum = bias_total[...].sum(axis=0, keepdims=True)
    place = lax.broadcasted_iota(jnp.int32, (8, chans), 0)
    parts_count, deep = keep.shape[0], keep.shape[1] - 8
    for ref, side in ((keep, core), (give, 1 - core)):
        for j in range(parts_count):
            at = pl.multiple_of((side * parts_count + j) * deep, 8)
            ref[j, :deep, :] = total[pl.ds(at, deep), :].astype(ref.dtype)
            tail = jnp.where((place == 0) & (side == 0), bias_sum, 0.0) if j == 0 else jnp.zeros((8, chans), F32)
            ref[j, deep:, :] = tail.astype(ref.dtype)


def back_kernel(part, halves, flags, grad, weights, *refs):
    out, wide, end, lines_out, sem = refs[-5:]
    slots, width, chans = grad.shape[1:]
    rows, cols = slots - 2, width - 8
    deep = rows // halves
    b, half = part // halves, part % halves
    start = half * deep
    step = 8
    is_north, is_south = flags[0], flags[1]

    def put(line, ref, index):
        line = line.astype(F32)
        ref[(*index, slice(None), slice(0, chans))] = pltpu.roll(line, 1, 0)[:cols].astype(BF16)
        ref[(*index, slice(None), slice(chans, 2 * chans))] = line[:cols].astype(BF16)
        ref[(*index, slice(None), slice(2 * chans, 3 * chans))] = pltpu.roll(line, width - 1, 0)[:cols].astype(BF16)

    edges = []
    for t, (own, slot, local_slot) in enumerate(((half == 0, 0, 0), (half == halves - 1, slots - 1, deep + 1))):
        if own:
            put(grad[b, slot], end, (t,))
            wide[local_slot] = jnp.zeros_like(wide[local_slot])
            tap = jnp.where(is_north == 1, 0, 2) if t == 0 else jnp.where(is_south == 1, 2, 0)
            edges.append(jnp.dot(end[t], weights[tap], preferred_element_type=F32))
        else:
            edges.append(None)
            put(grad[b, start + local_slot], wide, (local_slot,))
    for k in range(1, deep + 1):
        put(grad[b, start + k], wide, (k,))

    for first in range(0, deep, step):
        total = None
        for r in range(3):
            lines = wide[first + 2 - r : first + 2 - r + step, :, :].reshape(step * cols, 3 * chans)
            term = jnp.dot(lines, weights[r], preferred_element_type=F32)
            total = term if total is None else total + term
        total = total.reshape(step, cols, chans)
        for k in range(step):
            line = total[k]
            if first + k == 0 and edges[0] is not None:
                line = line + edges[0]
            if first + k == deep - 1 and edges[1] is not None:
                line = line + edges[1]
            lines_out[first + k] = line.astype(BF16)
    copy = pltpu.make_async_copy(lines_out, out.at[b, start : start + deep], sem)
    copy.start()
    copy.wait()


def finish_kernel(flags, mine, other, grad_kernel, grad_bias):
    parts, deep = mine.shape[0], mine.shape[1] - 8
    core = flags[3]
    for ref, side in ((mine, core), (other, 1 - core)):
        for j in range(parts):
            at = pl.multiple_of((side * parts + j) * deep, 8)
            grad_kernel[pl.ds(at, deep), :] = ref[j, :deep, :].astype(F32)
    first = jnp.where(core == 0, mine[0, deep:, :].astype(F32), other[0, deep:, :].astype(F32))
    grad_bias[...] = first[:1]


def circle(lats, lons):
    half = lons // 2
    fore = []
    for a in range(lats):
        for l in range(lons):
            if l < half:
                to = (a + 1, l) if a < lats - 1 else (a, l + half)
            else:
                to = (a - 1, l) if a > 0 else (a, l - half)
            fore.append((a * lons + l, to[0] * lons + to[1]))
    return fore, [(j, i) for i, j in fore]


def row_pair(field, at0, at1):
    return jnp.concatenate(
        [lax.dynamic_slice_in_dim(field, at0, 1, 1), lax.dynamic_slice_in_dim(field, at1, 1, 1)], axis=1
    )


def near(x):
    return pltpu.with_memory_space_constraint(x, pltpu.VMEM)


def vmem():
    return pl.BlockSpec(memory_space=pltpu.VMEM)


def local(fields, kernel, conv_bias, cotangent):
    batches, rows, cols, chans = fields.shape
    lat_count, lon_count = lax.axis_size(LAT), lax.axis_size(LON)
    lat, lon = lax.axis_index(LAT), lax.axis_index(LON)
    first_half = lon < lon_count // 2
    is_north, is_south = lat == 0, lat == lat_count - 1
    pairs, halves = rows // 2, cols // 2

    low = (jnp.where(is_south, rows - 1, rows - 2), jnp.where(is_south, rows - 2, rows - 1), pairs - 1)
    high = (jnp.where(is_north, 1, 0), jnp.where(is_north, 0, 1), 0)

    def message(down):
        at = [jnp.where(down, x, y) for x, y in zip(low, high)]
        return jnp.concatenate(
            [
                row_pair(fields, at[0], at[1]).reshape(batches, 2 * cols, chans),
                lax.dynamic_slice_in_dim(cotangent, at[2], 1, 1).reshape(batches, halves, chans),
            ],
            axis=1,
        )

    fore, aft = circle(lat_count, lon_count)
    from_fore = lax.ppermute(message(first_half), LAT + LON, fore)
    from_aft = lax.ppermute(message(~first_half), LAT + LON, aft)
    top = jnp.where(first_half, from_fore, from_aft)
    bottom = jnp.where(first_half, from_aft, from_fore)

    def column(c):
        return [
            top[:, c : c + 1], top[:, cols + c : cols + c + 1], fields[:, :, c],
            bottom[:, c : c + 1], bottom[:, cols + c : cols + c + 1],
        ]

    def cot_column(c):
        at = 2 * cols + c
        return [top[:, at : at + 1], cotangent[:, :, c], bottom[:, at : at + 1]]

    to_left = jnp.concatenate(column(0) + column(1) + cot_column(0), axis=1)
    to_right = jnp.concatenate(column(cols - 2) + column(cols - 1) + cot_column(halves - 1), axis=1)
    ring = [(i, (i + 1) % lon_count) for i in range(lon_count)]
    from_left = lax.ppermute(to_right, LON, ring)
    from_right = lax.ppermute(to_left, LON, [(j, i) for i, j in ring])

    total_rows = rows * lat_count
    index = jnp.clip(lat * rows - 1 + jnp.arange(rows + 2), 0, total_rows - 1)

    def cosine(at):
        return jnp.cos((at.astype(F32) + 0.5) * (math.pi / total_rows) - math.pi / 2)

    even = index // 2 * 2
    share = cosine(index) / (2.0 * (cosine(even) + cosine(even + 1)))
    core = lax.axis_index("core")
    flags = jnp.stack([is_north, is_south, first_half, core == 1]).astype(jnp.int32)

    weights = kernel.reshape(3, 3 * chans, chans)
    back_weights = jnp.swapaxes(kernel.reshape(3, 3, chans, chans)[:, ::-1], 2, 3).reshape(3, 3 * chans, chans)
    weights, back_weights, from_right = lax.optimization_barrier((weights, back_weights, from_right))
    plane = lax.axis_size(PLANE)
    deep = 9 * chans // (2 * plane)
    smem = pl.BlockSpec(memory_space=pltpu.SMEM)
    message_type = pltpu.VMEM((plane, deep + 8, chans), BF16)
    count = from_right.shape[1]
    pooled, grad, keep, give = pl.pallas_call(
        forward_kernel,
        out_shape=(
            jax.ShapeDtypeStruct((batches, pairs, halves, chans), BF16),
            pltpu.VMEM((batches, rows + 2, cols + 8, chans), BF16),
            message_type,
            message_type,
        ),
        in_specs=[smem, smem] + [vmem()] * 8,
        out_specs=[vmem()] * 4,
        scratch_shapes=[
            pltpu.VMEM((batches, rows + 4, cols + 8, 3 * chans), BF16),
            pltpu.VMEM((batches, count, chans), F32),
            pltpu.VMEM((batches, count, chans), F32),
            pltpu.VMEM((4, chans // 128, cols, 128), F32),
            pltpu.VMEM((4, chans // 128, cols, 128), F32),
            pltpu.VMEM((chans, batches * rows * cols), BF16),
            pltpu.VMEM((9 * chans, chans), F32),
            pltpu.VMEM((8, chans), F32),
        ],
        compiler_params=pltpu.CompilerParams(vmem_limit_bytes=56 << 20),
        name="forward",
    )(
        flags, share, fields, near(from_fore), near(from_aft), near(from_right), near(from_left),
        cotangent, weights, conv_bias[None],
    )

    parts_rows = rows // HALVES

    def back_part(part, back):
        held = () if back is None else (back,)
        return pl.pallas_call(
            functools.partial(back_kernel, part, HALVES),
            out_shape=jax.ShapeDtypeStruct((batches, rows, cols, chans), BF16),
            in_specs=[smem, vmem(), vmem()] + [pl.BlockSpec(memory_space=pl.ANY)] * len(held),
            out_specs=pl.BlockSpec(memory_space=pl.ANY),
            scratch_shapes=[
                pltpu.VMEM((parts_rows + 2, cols, 3 * chans), BF16),
                pltpu.VMEM((2, cols, 3 * chans), BF16),
                pltpu.VMEM((parts_rows, cols, chans), BF16),
                pltpu.SemaphoreType.DMA,
            ],
            input_output_aliases={3: 0} if held else {},
            cost_estimate=pl.CostEstimate(
                flops=2 * 9 * parts_rows * cols * chans * chans, transcendentals=0, bytes_accessed=parts_rows * cols * chans * 4
            ),
            compiler_params=pltpu.CompilerParams(vmem_limit_bytes=10 << 20),
            name="back",
        )(flags, near(grad), near(back_weights), *held)

    back = None
    for part in range(batches * HALVES):
        back = back_part(part, back)

    take = lax.ppermute(give, "core", [(0, 1), (1, 0)])
    part = (keep.astype(F32) + take.astype(F32)).astype(BF16)
    part = lax.all_to_all(part, PLANE, 0, 0, tiled=True)
    part = part.astype(F32).sum(axis=0).astype(BF16)
    size = lax.axis_size(RING)
    total = part.astype(F32)
    for k in range(1, size):
        away = lax.ppermute(part, RING, [(i, (i + k) % size) for i in range(size)])
        total = total + away.astype(F32)
    total = jnp.broadcast_to(total.astype(BF16)[None], (plane, deep + 8, chans))
    total = lax.all_to_all(total, PLANE, 0, 0, tiled=True)
    other = lax.ppermute(total, "core", [(0, 1), (1, 0)])
    grad_kernel, grad_bias = pl.pallas_call(
        finish_kernel,
        out_shape=(jax.ShapeDtypeStruct((9 * chans, chans), F32), jax.ShapeDtypeStruct((1, chans), F32)),
        in_specs=[smem, vmem(), vmem()],
        out_specs=[vmem()] * 2,
        compiler_params=pltpu.CompilerParams(vmem_limit_bytes=10 << 20),
        name="finish",
    )(flags, near(total), near(other))
    grad_kernel = grad_kernel.reshape(9, chans, chans)
    grad_bias = grad_bias.reshape(chans)
    return pooled, back, grad_kernel, grad_bias


def solution(mesh):
    lats, lons = mesh.devices.shape
    fine = Mesh(mesh.devices.reshape(2, lats // 2, lons // 4, 2, 2), LAT + LON)
    spec = P(None, LAT, LON, None)
    return jax.shard_map(
        local,
        mesh=fine,
        in_specs=(spec, P(), P(), spec),
        out_specs=(spec, spec, P(), P()),
        check_vma=False,
    )
```

```python
import functools
import math

import jax
import jax.numpy as jnp
from jax import lax
from jax.experimental import pallas as pl
from jax.experimental.pallas import tpu as pltpu
from jax.sharding import Mesh, PartitionSpec as P


F32 = jnp.float32
BF16 = jnp.bfloat16
HALVES = 2
LAT = ("yh", "z")
LON = ("x", "yl", "core")
RING = ("yh", "yl")
PLANE = ("x", "z")


def edge_block(right0, right1, left0, left1, chans):
    place = lax.broadcasted_iota(jnp.int32, (8, chans), 0)
    return jnp.where(
        place == 0,
        right0,
        jnp.where(place == 1, right1, jnp.where(place == 6, left0, jnp.where(place == 7, left1, 0.0))),
    )


def forward_kernel(
    flags, share, field, from_fore, from_aft, from_right, from_left, cot, weights, bias,
    pooled, grad, keep, give, wide, right, left, spread, pool, flipped, total, bias_total,
):
    batches, rows, cols, chans = field.shape
    width = cols + 8
    pairs = rows // 2
    step = 8
    is_north, is_south, first_half, core = flags[0], flags[1], flags[2], flags[3]
    right[...] = from_right[...].astype(F32)
    left[...] = from_left[...].astype(F32)
    span = rows + 4

    def put(b, e, own):
        edge = edge_block(
            right[b, pl.ds(e, 1), :], right[b, pl.ds(span + e, 1), :],
            left[b, pl.ds(e, 1), :], left[b, pl.ds(span + e, 1), :], chans,
        )
        line = jnp.concatenate([own, edge], axis=0)
        wide[b, e, :, :chans] = pltpu.roll(line, 1, 0).astype(BF16)
        wide[b, e, :, chans : 2 * chans] = line.astype(BF16)
        wide[b, e, :, 2 * chans :] = pltpu.roll(line, width - 1, 0).astype(BF16)

    def halo(b, lo, hi):
        fore = from_fore[b, lo:hi, :].astype(F32)
        aft = from_aft[b, lo:hi, :].astype(F32)
        top = jnp.where(first_half == 1, fore, aft)
        bottom = jnp.where(first_half == 1, aft, fore)
        return top, bottom

    for b in range(batches):
        for k in range(2):
            top, bottom = halo(b, k * cols, (k + 1) * cols)
            put(b, k, top)
            put(b, rows + 2 + k, bottom)

        def fill(i, carry):
            put(b, i + 2, field[b, i].astype(F32))
            return carry

        lax.fori_loop(0, rows, fill, 0, unroll=4)

    def conv(parts):
        acc = None
        for r in range(3):
            term = jnp.dot(parts[r], weights[r], preferred_element_type=F32)
            acc = term if acc is None else acc + term
        return acc + bias[...]

    def slope(pre):
        sigma = 0.5 + 0.5 * jnp.tanh(0.5 * pre)
        return sigma, sigma * (1.0 + pre * (1.0 - sigma))

    def join(ref, slot, at):
        return jnp.concatenate([ref[slot, h, at, :] for h in range(chans // 128)], axis=-1)

    def lift(slot, b, q, own):
        for h in range(chans // 128):
            for k in range(2):
                spread[slot, h, pl.ds(k, cols // 2, stride=2), :] = own[:, h * 128 : h * 128 + 128]
        place = lax.broadcasted_iota(jnp.int32, (8, chans), 0)
        edge = jnp.where(
            place == 0,
            right[b, pl.ds(2 * span + q, 1), :],
            jnp.where(place == 7, left[b, pl.ds(2 * span + q, 1), :], 0.0),
        )
        return jnp.concatenate([join(spread, slot, slice(0, cols)), edge], axis=0)

    for t in range(2):
        base = 0 if t == 0 else rows + 1
        turned = is_north if t == 0 else is_south
        parts = []
        for r in range(3):
            at = base + jnp.where(turned == 1, 2 - r, r)
            parts.append(wide[:, pl.ds(at, 1), :, :].reshape(batches * width, 3 * chans))
        _, rate = slope(conv(parts))
        for b in range(batches):
            cot_rows = halo(b, 2 * cols, 2 * cols + cols // 2)[t]
            value = lift(0, b, 0 if t == 0 else pairs + 1, cot_rows) * share[0 if t == 0 else rows + 1] * rate[b * width : (b + 1) * width]
            grad[b, 0 if t == 0 else rows + 1] = value.astype(BF16)

    bias_total[...] = jnp.zeros_like(bias_total)
    blocks = rows // step

    def block(n, carry):
        b = n // blocks
        first = (n % blocks) * step
        parts = [
            wide[b, pl.ds(first + 1 + r, step), :, :].reshape(step * width, 3 * chans) for r in range(3)
        ]
        pre = conv(parts)
        sigma, rate = slope(pre)
        active = (pre * sigma).reshape(step, width, chans)
        rate = rate.reshape(step, width, chans)
        lines = []
        for m in range(step // 2):
            q = first // 2 + m
            up, low = share[first + 2 * m + 1], share[first + 2 * m + 2]
            mixed = (active[2 * m] * up + active[2 * m + 1] * low)[:cols]
            for h in range(chans // 128):
                pool[m, h] = mixed[:, h * 128 : h * 128 + 128]
            even, odd = (join(pool, m, pl.ds(k, cols // 2, stride=2)) for k in range(2))
            pooled[b, q] = (even + odd).astype(BF16)
            lifted = lift(m, b, q + 1, cot[b, q].astype(F32))
            for k, part in ((2 * m, up), (2 * m + 1, low)):
                value = (lifted * part * rate[k]).astype(BF16)
                grad[b, first + k + 1] = value
                lines.append(value[:cols])
        own = jnp.concatenate(lines, axis=0)
        bias_total[...] += own.astype(F32).reshape(-1, 8, chans).sum(axis=0)
        at = pl.multiple_of(n * (step * cols), 128)
        flipped[:, pl.ds(at, step * cols)] = own.T
        return carry

    lax.fori_loop(0, batches * blocks, block, 0, unroll=True)

    size = rows * cols
    for r in range(3):
        acc = None
        for b in range(batches):
            term = jnp.dot(
                flipped[:, b * size : (b + 1) * size],
                wide[b, 1 + r : 1 + r + rows, :cols, :].reshape(size, 3 * chans),
                preferred_element_type=F32,
            )
            acc = term if acc is None else acc + term
        total[r * 3 * chans : (r + 1) * 3 * chans, :] = acc.T
    bias_sum = bias_total[...].sum(axis=0, keepdims=True)
    place = lax.broadcasted_iota(jnp.int32, (8, chans), 0)
    parts_count, deep = keep.shape[0], keep.shape[1] - 8
    for ref, side in ((keep, core), (give, 1 - core)):
        for j in range(parts_count):
            at = pl.multiple_of((side * parts_count + j) * deep, 8)
            ref[j, :deep, :] = total[pl.ds(at, deep), :].astype(ref.dtype)
            tail = jnp.where((place == 0) & (side == 0), bias_sum, 0.0) if j == 0 else jnp.zeros((8, chans), F32)
            ref[j, deep:, :] = tail.astype(ref.dtype)


def back_kernel(part, halves, flags, grad, weights, *refs):
    last = part == grad.shape[0] * halves - 1
    if last:
        out, flushed, wide, end, sem = refs[-5:]
    else:
        out, wide, end = refs[-3:]
    slots, width, chans = grad.shape[1:]
    rows, cols = slots - 2, width - 8
    deep = rows // halves
    b, half = part // halves, part % halves
    start = half * deep
    step = 8
    is_north, is_south = flags[0], flags[1]
    copies = []
    if last:
        for n, at in enumerate(((slice(0, b),), (b, slice(0, start)))):
            copies.append(pltpu.make_async_copy(out.at[at], flushed.at[at], sem.at[n]))
            copies[-1].start()

    def put(line, ref, index):
        line = line.astype(F32)
        ref[(*index, slice(None), slice(0, chans))] = pltpu.roll(line, 1, 0)[:cols].astype(BF16)
        ref[(*index, slice(None), slice(chans, 2 * chans))] = line[:cols].astype(BF16)
        ref[(*index, slice(None), slice(2 * chans, 3 * chans))] = pltpu.roll(line, width - 1, 0)[:cols].astype(BF16)

    edges = []
    for t, (own, slot, local_slot) in enumerate(((half == 0, 0, 0), (half == halves - 1, slots - 1, deep + 1))):
        if own:
            put(grad[b, slot], end, (t,))
            wide[local_slot] = jnp.zeros_like(wide[local_slot])
            tap = jnp.where(is_north == 1, 0, 2) if t == 0 else jnp.where(is_south == 1, 2, 0)
            edges.append(jnp.dot(end[t], weights[tap], preferred_element_type=F32))
        else:
            edges.append(None)
            put(grad[b, start + local_slot], wide, (local_slot,))
    for k in range(1, deep + 1):
        put(grad[b, start + k], wide, (k,))

    for first in range(0, deep, step):
        total = None
        for r in range(3):
            lines = wide[first + 2 - r : first + 2 - r + step, :, :].reshape(step * cols, 3 * chans)
            term = jnp.dot(lines, weights[r], preferred_element_type=F32)
            total = term if total is None else total + term
        total = total.reshape(step, cols, chans)
        for k in range(step):
            line = total[k]
            if first + k == 0 and edges[0] is not None:
                line = line + edges[0]
            if first + k == deep - 1 and edges[1] is not None:
                line = line + edges[1]
            out[b, start + first + k] = line.astype(BF16)
    for copy in copies:
        copy.wait()


def sum_kernel(parts, out):
    total = parts[0].astype(F32)
    for k in range(1, parts.shape[0]):
        total = total + parts[k].astype(F32)
    out[...] = total.astype(out.dtype)


def finish_kernel(flags, mine, other, back, flushed, grad_kernel, grad_bias, back_out, lines, sem):
    parts, deep = mine.shape[0], mine.shape[1] - 8
    core = flags[3]
    at = (back.shape[0] - 1, slice(back.shape[1] // HALVES * (HALVES - 1), back.shape[1]))
    copies = [pltpu.make_async_copy(back.at[at], back_out.at[at], sem.at[0])]
    copies[0].start()
    steps = 2
    many = parts // steps
    for n, (ref, side) in enumerate(((mine, core), (other, 1 - core))):
        for k in range(steps):
            first = n * parts + k * many
            for j in range(many):
                lines[(first + j) * deep : (first + j + 1) * deep, :] = ref[k * many + j, :deep, :].astype(F32)
            at = pl.multiple_of((side * parts + k * many) * deep, 8)
            copy = pltpu.make_async_copy(
                lines.at[first * deep : (first + many) * deep],
                grad_kernel.at[pl.ds(at, many * deep)],
                sem.at[1 + n * steps + k],
            )
            copy.start()
            copies.append(copy)
    first = jnp.where(core == 0, mine[0, deep:, :].astype(F32), other[0, deep:, :].astype(F32))
    grad_bias[...] = first[:1]
    for copy in copies:
        copy.wait()


def circle(lats, lons):
    half = lons // 2
    fore = []
    for a in range(lats):
        for l in range(lons):
            if l < half:
                to = (a + 1, l) if a < lats - 1 else (a, l + half)
            else:
                to = (a - 1, l) if a > 0 else (a, l - half)
            fore.append((a * lons + l, to[0] * lons + to[1]))
    return fore, [(j, i) for i, j in fore]


def row_pair(field, at0, at1):
    return jnp.concatenate(
        [lax.dynamic_slice_in_dim(field, at0, 1, 1), lax.dynamic_slice_in_dim(field, at1, 1, 1)], axis=1
    )


def near(x):
    return pltpu.with_memory_space_constraint(x, pltpu.VMEM)


def vmem():
    return pl.BlockSpec(memory_space=pltpu.VMEM)


def local(fields, kernel, conv_bias, cotangent):
    batches, rows, cols, chans = fields.shape
    lat_count, lon_count = lax.axis_size(LAT), lax.axis_size(LON)
    lat, lon = lax.axis_index(LAT), lax.axis_index(LON)
    first_half = lon < lon_count // 2
    is_north, is_south = lat == 0, lat == lat_count - 1
    pairs, halves = rows // 2, cols // 2

    low = (jnp.where(is_south, rows - 1, rows - 2), jnp.where(is_south, rows - 2, rows - 1), pairs - 1)
    high = (jnp.where(is_north, 1, 0), jnp.where(is_north, 0, 1), 0)

    def message(down):
        at = [jnp.where(down, x, y) for x, y in zip(low, high)]
        return jnp.concatenate(
            [
                row_pair(fields, at[0], at[1]).reshape(batches, 2 * cols, chans),
                lax.dynamic_slice_in_dim(cotangent, at[2], 1, 1).reshape(batches, halves, chans),
            ],
            axis=1,
        )

    fore, aft = circle(lat_count, lon_count)
    from_fore = lax.ppermute(message(first_half), LAT + LON, fore)
    from_aft = lax.ppermute(message(~first_half), LAT + LON, aft)
    top = jnp.where(first_half, from_fore, from_aft)
    bottom = jnp.where(first_half, from_aft, from_fore)

    def column(c):
        return [
            top[:, c : c + 1], top[:, cols + c : cols + c + 1], fields[:, :, c],
            bottom[:, c : c + 1], bottom[:, cols + c : cols + c + 1],
        ]

    def cot_column(c):
        at = 2 * cols + c
        return [top[:, at : at + 1], cotangent[:, :, c], bottom[:, at : at + 1]]

    to_left = jnp.concatenate(column(0) + column(1) + cot_column(0), axis=1)
    to_right = jnp.concatenate(column(cols - 2) + column(cols - 1) + cot_column(halves - 1), axis=1)
    ring = [(i, (i + 1) % lon_count) for i in range(lon_count)]
    from_left = lax.ppermute(to_right, LON, ring)
    from_right = lax.ppermute(to_left, LON, [(j, i) for i, j in ring])

    total_rows = rows * lat_count
    index = jnp.clip(lat * rows - 1 + jnp.arange(rows + 2), 0, total_rows - 1)

    def cosine(at):
        return jnp.cos((at.astype(F32) + 0.5) * (math.pi / total_rows) - math.pi / 2)

    even = index // 2 * 2
    share = cosine(index) / (2.0 * (cosine(even) + cosine(even + 1)))
    core = lax.axis_index("core")
    flags = jnp.stack([is_north, is_south, first_half, core == 1]).astype(jnp.int32)

    weights = kernel.reshape(3, 3 * chans, chans)
    back_weights = jnp.swapaxes(kernel.reshape(3, 3, chans, chans)[:, ::-1], 2, 3).reshape(3, 3 * chans, chans)
    weights, back_weights, from_right = lax.optimization_barrier((weights, back_weights, from_right))
    plane = lax.axis_size(PLANE)
    deep = 9 * chans // (2 * plane)
    smem = pl.BlockSpec(memory_space=pltpu.SMEM)
    message_type = pltpu.VMEM((plane, deep + 8, chans), BF16)
    count = from_right.shape[1]
    pooled, grad, keep, give = pl.pallas_call(
        forward_kernel,
        out_shape=(
            jax.ShapeDtypeStruct((batches, pairs, halves, chans), BF16),
            pltpu.VMEM((batches, rows + 2, cols + 8, chans), BF16),
            message_type,
            message_type,
        ),
        in_specs=[smem, smem] + [vmem()] * 8,
        out_specs=[vmem()] * 4,
        scratch_shapes=[
            pltpu.VMEM((batches, rows + 4, cols + 8, 3 * chans), BF16),
            pltpu.VMEM((batches, count, chans), F32),
            pltpu.VMEM((batches, count, chans), F32),
            pltpu.VMEM((4, chans // 128, cols, 128), F32),
            pltpu.VMEM((4, chans // 128, cols, 128), F32),
            pltpu.VMEM((chans, batches * rows * cols), BF16),
            pltpu.VMEM((9 * chans, chans), F32),
            pltpu.VMEM((8, chans), F32),
        ],
        compiler_params=pltpu.CompilerParams(vmem_limit_bytes=56 << 20),
        name="forward",
    )(
        flags, share, fields, near(from_fore), near(from_aft), near(from_right), near(from_left),
        cotangent, weights, conv_bias[None],
    )

    parts_rows = rows // HALVES

    parts = batches * HALVES

    def back_part(part, back):
        held = () if back is None else (near(back),)
        ends = part == parts - 1
        result = pltpu.VMEM(fields.shape, BF16)
        hbm = pl.BlockSpec(memory_space=pl.ANY)
        return pl.pallas_call(
            functools.partial(back_kernel, part, HALVES),
            out_shape=(result, jax.ShapeDtypeStruct(fields.shape, BF16)) if ends else result,
            in_specs=[smem, vmem(), vmem()] + [vmem()] * len(held),
            out_specs=(vmem(), hbm) if ends else vmem(),
            scratch_shapes=[
                pltpu.VMEM((parts_rows + 2, cols, 3 * chans), BF16),
                pltpu.VMEM((2, cols, 3 * chans), BF16),
            ] + [pltpu.SemaphoreType.DMA((2,))] * ends,
            input_output_aliases={3: 0} if held else {},
            compiler_params=pltpu.CompilerParams(vmem_limit_bytes=10 << 20),
            cost_estimate=pl.CostEstimate(
                flops=2 * 9 * parts_rows * cols * chans * chans, transcendentals=0, bytes_accessed=parts_rows * cols * chans * 4
            ),
            name="back",
        )(flags, near(grad), near(back_weights), *held)

    back = None
    for part in range(parts):
        back = back_part(part, back)
    back, flushed = back

    take = lax.ppermute(give, "core", [(0, 1), (1, 0)])
    part = (keep.astype(F32) + take.astype(F32)).astype(BF16)
    part = lax.all_to_all(part, PLANE, 0, 0, tiled=True)
    part = pl.pallas_call(
        sum_kernel,
        out_shape=jax.ShapeDtypeStruct(part.shape[1:], BF16),
        in_specs=[vmem()],
        out_specs=vmem(),
        compiler_params=pltpu.CompilerParams(vmem_limit_bytes=10 << 20),
        name="sum",
    )(near(part))
    size = lax.axis_size(RING)
    total = part.astype(F32)
    for k in range(1, size):
        away = lax.ppermute(part, RING, [(i, (i + k) % size) for i in range(size)])
        total = total + away.astype(F32)
    total = jnp.broadcast_to(total.astype(BF16)[None], (plane, deep + 8, chans))
    total = lax.all_to_all(total, PLANE, 0, 0, tiled=True)
    other = lax.ppermute(total, "core", [(0, 1), (1, 0)])

    grad_kernel, grad_bias, back = pl.pallas_call(
        finish_kernel,
        out_shape=(
            jax.ShapeDtypeStruct((9 * chans, chans), F32),
            jax.ShapeDtypeStruct((1, chans), F32),
            jax.ShapeDtypeStruct(fields.shape, BF16),
        ),
        in_specs=[smem] + [vmem()] * 3 + [pl.BlockSpec(memory_space=pl.ANY)],
        out_specs=[pl.BlockSpec(memory_space=pl.ANY), vmem(), pl.BlockSpec(memory_space=pl.ANY)],
        scratch_shapes=[pltpu.VMEM((9 * chans, chans), F32), pltpu.SemaphoreType.DMA((5,))],
        input_output_aliases={4: 2},
        compiler_params=pltpu.CompilerParams(vmem_limit_bytes=10 << 20),
        name="finish",
    )(flags, near(total), near(other), near(back), flushed)
    grad_kernel = grad_kernel.reshape(9, chans, chans)
    grad_bias = grad_bias.reshape(chans)
    return pooled, back, grad_kernel, grad_bias


def solution(mesh):
    lats, lons = mesh.devices.shape
    fine = Mesh(mesh.devices.reshape(2, lats // 2, lons // 4, 2, 2), LAT + LON)
    spec = P(None, LAT, LON, None)
    return jax.shard_map(
        local,
        mesh=fine,
        in_specs=(spec, P(), P(), spec),
        out_specs=(spec, spec, P(), P()),
        check_vma=False,
    )
```

```python
import functools
import math

import jax
import jax.numpy as jnp
from jax import lax
from jax.experimental import pallas as pl
from jax.experimental.pallas import tpu as pltpu
from jax.sharding import Mesh, PartitionSpec as P


F32 = jnp.float32
BF16 = jnp.bfloat16
HALVES = 2
LAT = ("yh", "z")
LON = ("x", "yl", "core")
RING = ("yh", "yl")
PLANE = ("x", "z")


def edge_block(right0, right1, left0, left1, chans):
    place = lax.broadcasted_iota(jnp.int32, (8, chans), 0)
    return jnp.where(
        place == 0,
        right0,
        jnp.where(place == 1, right1, jnp.where(place == 6, left0, jnp.where(place == 7, left1, 0.0))),
    )


def put_line(wide, b, e, line):
    width, chans = line.shape
    wide[b, e, :, :chans] = pltpu.roll(line, 1, 0).astype(BF16)
    wide[b, e, :, chans : 2 * chans] = line.astype(BF16)
    wide[b, e, :, 2 * chans :] = pltpu.roll(line, width - 1, 0).astype(BF16)


def prepare_kernel(kernel, weights, back_weights):
    chans = kernel.shape[-1]
    for r in range(3):
        for s in range(3):
            tap = kernel[3 * r + s]
            weights[r, s * chans : (s + 1) * chans, :] = tap
            back_weights[r, (2 - s) * chans : (3 - s) * chans, :] = tap.T


def fill_kernel(field, cot, wide, cot_out):
    batches, rows, _, chans = field.shape
    blank = jnp.zeros((8, chans), F32)
    for b in range(batches):

        def fill(i, carry):
            put_line(wide, b, i + 2, jnp.concatenate([field[b, i].astype(F32), blank], axis=0))
            return carry

        lax.fori_loop(0, rows, fill, 0, unroll=4)
    cot_out[...] = cot[...]


def forward_kernel(
    flags, share, filled, from_fore, from_aft, from_right, from_left, cot, weights, bias,
    pooled, grad, keep, give, wide, right, left, spread, pool, flipped, total, bias_total,
):
    batches, slots, width, chans = wide.shape
    chans //= 3
    rows, cols = slots - 4, width - 8
    pairs = rows // 2
    step = 8
    is_north, is_south, first_half, core = flags[0], flags[1], flags[2], flags[3]
    right[...] = from_right[...].astype(F32)
    left[...] = from_left[...].astype(F32)
    span = rows + 4

    place8 = lax.broadcasted_iota(jnp.int32, (8, chans), 0)

    def edge_of(b, e):
        return edge_block(
            right[b, pl.ds(e, 1), :], right[b, pl.ds(span + e, 1), :],
            left[b, pl.ds(e, 1), :], left[b, pl.ds(span + e, 1), :], chans,
        )

    def put(b, e, own):
        put_line(wide, b, e, jnp.concatenate([own, edge_of(b, e)], axis=0))

    def patch(b, e):
        edge = edge_of(b, e)
        after, before = pltpu.roll(edge, 1, 0), pltpu.roll(edge, 7, 0)
        low, high = wide[b, e, :16, chans : 2 * chans], wide[b, e, cols - 16 : cols, chans : 2 * chans]
        up, down = wide[b, e, :16, :chans].astype(F32), wide[b, e, cols - 16 : cols, 2 * chans :].astype(F32)
        wide[b, e, cols:, :chans] = jnp.where(place8 == 0, pltpu.roll(high.astype(F32)[8:], 1, 0), after).astype(BF16)
        wide[b, e, cols:, chans : 2 * chans] = edge.astype(BF16)
        wide[b, e, cols:, 2 * chans :] = jnp.where(place8 == 7, pltpu.roll(low.astype(F32)[:8], 7, 0), before).astype(BF16)
        up = jnp.concatenate([jnp.where(place8 == 0, after, up[:8]), up[8:]], axis=0)
        down = jnp.concatenate([down[:8], jnp.where(place8 == 7, before, down[8:])], axis=0)
        wide[b, e, :16, :chans] = up.astype(BF16)
        wide[b, e, cols - 16 : cols, 2 * chans :] = down.astype(BF16)

    def halo(b, lo, hi):
        fore = from_fore[b, lo:hi, :].astype(F32)
        aft = from_aft[b, lo:hi, :].astype(F32)
        top = jnp.where(first_half == 1, fore, aft)
        bottom = jnp.where(first_half == 1, aft, fore)
        return top, bottom

    for b in range(batches):
        for k in range(2):
            top, bottom = halo(b, k * cols, (k + 1) * cols)
            put(b, k, top)
            put(b, rows + 2 + k, bottom)

        def fill(i, carry):
            patch(b, i + 2)
            return carry

        lax.fori_loop(0, rows, fill, 0, unroll=4)

    def conv(parts):
        acc = None
        for r in range(3):
            term = jnp.dot(parts[r], weights[r], preferred_element_type=F32)
            acc = term if acc is None else acc + term
        return acc + bias[...]

    def slope(pre):
        sigma = 0.5 + 0.5 * jnp.tanh(0.5 * pre)
        return sigma, sigma * (1.0 + pre * (1.0 - sigma))

    def join(ref, slot, at):
        return jnp.concatenate([ref[slot, h, at, :] for h in range(chans // 128)], axis=-1)

    def lift(slot, b, q, own):
        for h in range(chans // 128):
            for k in range(2):
                spread[slot, h, pl.ds(k, cols // 2, stride=2), :] = own[:, h * 128 : h * 128 + 128]
        place = lax.broadcasted_iota(jnp.int32, (8, chans), 0)
        edge = jnp.where(
            place == 0,
            right[b, pl.ds(2 * span + q, 1), :],
            jnp.where(place == 7, left[b, pl.ds(2 * span + q, 1), :], 0.0),
        )
        return jnp.concatenate([join(spread, slot, slice(0, cols)), edge], axis=0)

    for t in range(2):
        base = 0 if t == 0 else rows + 1
        turned = is_north if t == 0 else is_south
        parts = []
        for r in range(3):
            at = base + jnp.where(turned == 1, 2 - r, r)
            parts.append(wide[:, pl.ds(at, 1), :, :].reshape(batches * width, 3 * chans))
        _, rate = slope(conv(parts))
        for b in range(batches):
            cot_rows = halo(b, 2 * cols, 2 * cols + cols // 2)[t]
            value = lift(0, b, 0 if t == 0 else pairs + 1, cot_rows) * share[0 if t == 0 else rows + 1] * rate[b * width : (b + 1) * width]
            grad[b, 0 if t == 0 else rows + 1] = value.astype(BF16)

    bias_total[...] = jnp.zeros_like(bias_total)
    blocks = rows // step

    def block(n, carry):
        b = n // blocks
        first = (n % blocks) * step
        parts = [
            wide[b, pl.ds(first + 1 + r, step), :, :].reshape(step * width, 3 * chans) for r in range(3)
        ]
        pre = conv(parts)
        sigma, rate = slope(pre)
        active = (pre * sigma).reshape(step, width, chans)
        rate = rate.reshape(step, width, chans)
        lines = []
        for m in range(step // 2):
            q = first // 2 + m
            up, low = share[first + 2 * m + 1], share[first + 2 * m + 2]
            mixed = (active[2 * m] * up + active[2 * m + 1] * low)[:cols]
            for h in range(chans // 128):
                pool[m, h] = mixed[:, h * 128 : h * 128 + 128]
            even, odd = (join(pool, m, pl.ds(k, cols // 2, stride=2)) for k in range(2))
            pooled[b, q] = (even + odd).astype(BF16)
            lifted = lift(m, b, q + 1, cot[b, q].astype(F32))
            for k, part in ((2 * m, up), (2 * m + 1, low)):
                value = (lifted * part * rate[k]).astype(BF16)
                grad[b, first + k + 1] = value
                lines.append(value[:cols])
        own = jnp.concatenate(lines, axis=0)
        bias_total[...] += own.astype(F32).reshape(-1, 8, chans).sum(axis=0)
        at = pl.multiple_of(n * (step * cols), 128)
        flipped[:, pl.ds(at, step * cols)] = own.T
        return carry

    lax.fori_loop(0, batches * blocks, block, 0, unroll=True)

    size = rows * cols
    for r in range(3):
        acc = None
        for b in range(batches):
            term = jnp.dot(
                flipped[:, b * size : (b + 1) * size],
                wide[b, 1 + r : 1 + r + rows, :cols, :].reshape(size, 3 * chans),
                preferred_element_type=F32,
            )
            acc = term if acc is None else acc + term
        total[r * 3 * chans : (r + 1) * 3 * chans, :] = acc.T
    bias_sum = bias_total[...].sum(axis=0, keepdims=True)
    place = lax.broadcasted_iota(jnp.int32, (8, chans), 0)
    parts_count, deep = keep.shape[0], keep.shape[1] - 8
    for ref, side in ((keep, core), (give, 1 - core)):
        for j in range(parts_count):
            at = pl.multiple_of((side * parts_count + j) * deep, 8)
            ref[j, :deep, :] = total[pl.ds(at, deep), :].astype(ref.dtype)
            tail = jnp.where((place == 0) & (side == 0), bias_sum, 0.0) if j == 0 else jnp.zeros((8, chans), F32)
            ref[j, deep:, :] = tail.astype(ref.dtype)


def back_kernel(part, halves, flags, grad, weights, *refs):
    last = part == grad.shape[0] * halves - 1
    if last:
        out, flushed, wide, end, sem = refs[-5:]
    else:
        out, wide, end = refs[-3:]
    slots, width, chans = grad.shape[1:]
    rows, cols = slots - 2, width - 8
    deep = rows // halves
    b, half = part // halves, part % halves
    start = half * deep
    step = 8
    is_north, is_south = flags[0], flags[1]
    copies = []
    if last:
        for n, at in enumerate(((slice(0, b),), (b, slice(0, start)))):
            copies.append(pltpu.make_async_copy(out.at[at], flushed.at[at], sem.at[n]))
            copies[-1].start()

    def put(line, ref, index):
        line = line.astype(F32)
        ref[(*index, slice(None), slice(0, chans))] = pltpu.roll(line, 1, 0)[:cols].astype(BF16)
        ref[(*index, slice(None), slice(chans, 2 * chans))] = line[:cols].astype(BF16)
        ref[(*index, slice(None), slice(2 * chans, 3 * chans))] = pltpu.roll(line, width - 1, 0)[:cols].astype(BF16)

    edges = []
    for t, (own, slot, local_slot) in enumerate(((half == 0, 0, 0), (half == halves - 1, slots - 1, deep + 1))):
        if own:
            put(grad[b, slot], end, (t,))
            wide[local_slot] = jnp.zeros_like(wide[local_slot])
            tap = jnp.where(is_north == 1, 0, 2) if t == 0 else jnp.where(is_south == 1, 2, 0)
            edges.append(jnp.dot(end[t], weights[tap], preferred_element_type=F32))
        else:
            edges.append(None)
            put(grad[b, start + local_slot], wide, (local_slot,))
    for k in range(1, deep + 1):
        put(grad[b, start + k], wide, (k,))

    for first in range(0, deep, step):
        total = None
        for r in range(3):
            lines = wide[first + 2 - r : first + 2 - r + step, :, :].reshape(step * cols, 3 * chans)
            term = jnp.dot(lines, weights[r], preferred_element_type=F32)
            total = term if total is None else total + term
        total = total.reshape(step, cols, chans)
        for k in range(step):
            line = total[k]
            if first + k == 0 and edges[0] is not None:
                line = line + edges[0]
            if first + k == deep - 1 and edges[1] is not None:
                line = line + edges[1]
            out[b, start + first + k] = line.astype(BF16)
    for copy in copies:
        copy.wait()


def sum_kernel(parts, out):
    total = parts[0].astype(F32)
    for k in range(1, parts.shape[0]):
        total = total + parts[k].astype(F32)
    out[...] = total.astype(out.dtype)


def finish_kernel(flags, mine, other, back, flushed, grad_kernel, grad_bias, back_out, lines, sem):
    parts, deep = mine.shape[0], mine.shape[1] - 8
    core = flags[3]
    at = (back.shape[0] - 1, slice(back.shape[1] // HALVES * (HALVES - 1), back.shape[1]))
    copies = [pltpu.make_async_copy(back.at[at], back_out.at[at], sem.at[0])]
    copies[0].start()
    steps = 2
    many = parts // steps
    for n, (ref, side) in enumerate(((mine, core), (other, 1 - core))):
        for k in range(steps):
            first = n * parts + k * many
            for j in range(many):
                lines[(first + j) * deep : (first + j + 1) * deep, :] = ref[k * many + j, :deep, :].astype(F32)
            at = pl.multiple_of((side * parts + k * many) * deep, 8)
            copy = pltpu.make_async_copy(
                lines.at[first * deep : (first + many) * deep],
                grad_kernel.at[pl.ds(at, many * deep)],
                sem.at[1 + n * steps + k],
            )
            copy.start()
            copies.append(copy)
    first = jnp.where(core == 0, mine[0, deep:, :].astype(F32), other[0, deep:, :].astype(F32))
    grad_bias[...] = first[:1]
    for copy in copies:
        copy.wait()


def circle(lats, lons):
    half = lons // 2
    fore = []
    for a in range(lats):
        for l in range(lons):
            if l < half:
                to = (a + 1, l) if a < lats - 1 else (a, l + half)
            else:
                to = (a - 1, l) if a > 0 else (a, l - half)
            fore.append((a * lons + l, to[0] * lons + to[1]))
    return fore, [(j, i) for i, j in fore]


def row_pair(field, at0, at1):
    return jnp.concatenate(
        [lax.dynamic_slice_in_dim(field, at0, 1, 1), lax.dynamic_slice_in_dim(field, at1, 1, 1)], axis=1
    )


def near(x):
    return pltpu.with_memory_space_constraint(x, pltpu.VMEM)


def vmem():
    return pl.BlockSpec(memory_space=pltpu.VMEM)


def local(fields, kernel, conv_bias, cotangent):
    batches, rows, cols, chans = fields.shape
    lat_count, lon_count = lax.axis_size(LAT), lax.axis_size(LON)
    lat, lon = lax.axis_index(LAT), lax.axis_index(LON)
    first_half = lon < lon_count // 2
    is_north, is_south = lat == 0, lat == lat_count - 1
    pairs, halves = rows // 2, cols // 2

    low = (jnp.where(is_south, rows - 1, rows - 2), jnp.where(is_south, rows - 2, rows - 1), pairs - 1)
    high = (jnp.where(is_north, 1, 0), jnp.where(is_north, 0, 1), 0)

    def message(down):
        at = [jnp.where(down, x, y) for x, y in zip(low, high)]
        return jnp.concatenate(
            [
                row_pair(fields, at[0], at[1]).reshape(batches, 2 * cols, chans),
                lax.dynamic_slice_in_dim(cotangent, at[2], 1, 1).reshape(batches, halves, chans),
            ],
            axis=1,
        )

    fore, aft = circle(lat_count, lon_count)
    from_fore = lax.ppermute(message(first_half), LAT + LON, fore)
    from_aft = lax.ppermute(message(~first_half), LAT + LON, aft)
    top = jnp.where(first_half, from_fore, from_aft)
    bottom = jnp.where(first_half, from_aft, from_fore)

    def column(c):
        return [
            top[:, c : c + 1], top[:, cols + c : cols + c + 1], fields[:, :, c],
            bottom[:, c : c + 1], bottom[:, cols + c : cols + c + 1],
        ]

    def cot_column(c):
        at = 2 * cols + c
        return [top[:, at : at + 1], cotangent[:, :, c], bottom[:, at : at + 1]]

    to_left = jnp.concatenate(column(0) + column(1) + cot_column(0), axis=1)
    to_right = jnp.concatenate(column(cols - 2) + column(cols - 1) + cot_column(halves - 1), axis=1)
    ring = [(i, (i + 1) % lon_count) for i in range(lon_count)]
    from_left = lax.ppermute(to_right, LON, ring)
    from_right = lax.ppermute(to_left, LON, [(j, i) for i, j in ring])

    total_rows = rows * lat_count
    index = jnp.clip(lat * rows - 1 + jnp.arange(rows + 2), 0, total_rows - 1)

    def cosine(at):
        return jnp.cos((at.astype(F32) + 0.5) * (math.pi / total_rows) - math.pi / 2)

    even = index // 2 * 2
    share = cosine(index) / (2.0 * (cosine(even) + cosine(even + 1)))
    core = lax.axis_index("core")
    flags = jnp.stack([is_north, is_south, first_half, core == 1]).astype(jnp.int32)

    weights_type = pltpu.VMEM((3, 3 * chans, chans), BF16)
    weights, back_weights = pl.pallas_call(
        prepare_kernel,
        out_shape=(weights_type, weights_type),
        in_specs=[vmem()],
        out_specs=[vmem()] * 2,
        compiler_params=pltpu.CompilerParams(vmem_limit_bytes=57 << 20),
        name="prepare",
    )(kernel)
    plane = lax.axis_size(PLANE)
    deep = 9 * chans // (2 * plane)
    smem = pl.BlockSpec(memory_space=pltpu.SMEM)
    message_type = pltpu.VMEM((plane, deep + 8, chans), BF16)
    count = from_right.shape[1]
    wide_type = pltpu.VMEM((batches, rows + 4, cols + 8, 3 * chans), BF16)
    wide, cot = pl.pallas_call(
        fill_kernel,
        out_shape=(wide_type, pltpu.VMEM(cotangent.shape, BF16)),
        in_specs=[vmem()] * 2,
        out_specs=[vmem()] * 2,
        compiler_params=pltpu.CompilerParams(vmem_limit_bytes=52 << 20),
        name="fill",
    )(fields, cotangent)
    pooled, grad, keep, give, _ = pl.pallas_call(
        forward_kernel,
        out_shape=(
            jax.ShapeDtypeStruct((batches, pairs, halves, chans), BF16),
            pltpu.VMEM((batches, rows + 2, cols + 8, chans), BF16),
            message_type,
            message_type,
            wide_type,
        ),
        in_specs=[smem, smem] + [vmem()] * 8,
        out_specs=[vmem()] * 5,
        input_output_aliases={2: 4},
        scratch_shapes=[
            pltpu.VMEM((batches, count, chans), F32),
            pltpu.VMEM((batches, count, chans), F32),
            pltpu.VMEM((4, chans // 128, cols, 128), F32),
            pltpu.VMEM((4, chans // 128, cols, 128), F32),
            pltpu.VMEM((chans, batches * rows * cols), BF16),
            pltpu.VMEM((9 * chans, chans), F32),
            pltpu.VMEM((8, chans), F32),
        ],
        compiler_params=pltpu.CompilerParams(vmem_limit_bytes=36 << 20),
        name="forward",
    )(
        flags, share, near(wide), near(from_fore), near(from_aft), near(from_right), near(from_left),
        near(cot), near(weights), conv_bias[None],
    )

    parts_rows = rows // HALVES

    parts = batches * HALVES

    def back_part(part, back):
        held = () if back is None else (near(back),)
        ends = part == parts - 1
        result = pltpu.VMEM(fields.shape, BF16)
        hbm = pl.BlockSpec(memory_space=pl.ANY)
        return pl.pallas_call(
            functools.partial(back_kernel, part, HALVES),
            out_shape=(result, jax.ShapeDtypeStruct(fields.shape, BF16)) if ends else result,
            in_specs=[smem, vmem(), vmem()] + [vmem()] * len(held),
            out_specs=(vmem(), hbm) if ends else vmem(),
            scratch_shapes=[
                pltpu.VMEM((parts_rows + 2, cols, 3 * chans), BF16),
                pltpu.VMEM((2, cols, 3 * chans), BF16),
            ] + [pltpu.SemaphoreType.DMA((2,))] * ends,
            input_output_aliases={3: 0} if held else {},
            compiler_params=pltpu.CompilerParams(vmem_limit_bytes=10 << 20),
            cost_estimate=pl.CostEstimate(
                flops=2 * 9 * parts_rows * cols * chans * chans, transcendentals=0, bytes_accessed=parts_rows * cols * chans * 4
            ),
            name="back",
        )(flags, near(grad), near(back_weights), *held)

    back = None
    for part in range(parts):
        back = back_part(part, back)
    back, flushed = back

    take = lax.ppermute(give, "core", [(0, 1), (1, 0)])
    part = (keep.astype(F32) + take.astype(F32)).astype(BF16)
    part = lax.all_to_all(part, PLANE, 0, 0, tiled=True)
    part = pl.pallas_call(
        sum_kernel,
        out_shape=jax.ShapeDtypeStruct(part.shape[1:], BF16),
        in_specs=[vmem()],
        out_specs=vmem(),
        compiler_params=pltpu.CompilerParams(vmem_limit_bytes=10 << 20),
        name="sum",
    )(near(part))
    size = lax.axis_size(RING)
    total = part.astype(F32)
    for k in range(1, size):
        away = lax.ppermute(part, RING, [(i, (i + k) % size) for i in range(size)])
        total = total + away.astype(F32)
    total = jnp.broadcast_to(total.astype(BF16)[None], (plane, deep + 8, chans))
    total = lax.all_to_all(total, PLANE, 0, 0, tiled=True)
    other = lax.ppermute(total, "core", [(0, 1), (1, 0)])

    grad_kernel, grad_bias, back = pl.pallas_call(
        finish_kernel,
        out_shape=(
            jax.ShapeDtypeStruct((9 * chans, chans), F32),
            jax.ShapeDtypeStruct((1, chans), F32),
            jax.ShapeDtypeStruct(fields.shape, BF16),
        ),
        in_specs=[smem] + [vmem()] * 3 + [pl.BlockSpec(memory_space=pl.ANY)],
        out_specs=[pl.BlockSpec(memory_space=pl.ANY), vmem(), pl.BlockSpec(memory_space=pl.ANY)],
        scratch_shapes=[pltpu.VMEM((9 * chans, chans), F32), pltpu.SemaphoreType.DMA((5,))],
        input_output_aliases={4: 2},
        compiler_params=pltpu.CompilerParams(vmem_limit_bytes=10 << 20),
        name="finish",
    )(flags, near(total), near(other), near(back), flushed)
    grad_kernel = grad_kernel.reshape(9, chans, chans)
    grad_bias = grad_bias.reshape(chans)
    return pooled, back, grad_kernel, grad_bias


def solution(mesh):
    lats, lons = mesh.devices.shape
    fine = Mesh(mesh.devices.reshape(2, lats // 2, lons // 4, 2, 2), LAT + LON)
    spec = P(None, LAT, LON, None)
    return jax.shard_map(
        local,
        mesh=fine,
        in_specs=(spec, P(), P(), spec),
        out_specs=(spec, spec, P(), P()),
        check_vma=False,
    )
```
